256 devices in a mesh: scene: 4 (over y), space: 64 (over z, x, core).
Axes of the slice: x: 4, y: 4, z: 8, core: 2. Of those that a mesh axis runs over, the one named last changes fastest.
Arguments:
- features: bfloat16 [4, 49152, 128], P('scene', 'space'), may hold values from -6 to 6
- cotangent: bfloat16 [4, 49152, 128], P('scene', 'space'), may hold values from -0.09375 to 0.09375
- conv_weight: bfloat16 [3456, 128], replicated, may hold values from -0.109375 to 0.109375
- down_weight: bfloat16 [1024, 256], replicated, may hold values from -0.1875 to 0.1875
- up_weight: bfloat16 [256, 1024], replicated, may hold values from -0.375 to 0.375
- live_count: int32 [4, 64], P('scene', 'space'), may hold values from 256 to 768, as said below
- neighbours: int32 [4, 26, 49152], P('scene', None, 'space'), may hold values from -1 to 959, as said below
- destination: int32 [4, 49152, 1], P('scene', 'space'), may hold values from 0 to 63; in each aligned block of 768 rows (0 to 767, 768 to 1535, ..., all dimensions but the last counted through in order) at most 24 rows name the same one
- assemble: int32 [4, 64, 1536], P('scene', 'space'), may hold values from 0 to 1535, each once within a row
Outputs:
- output: bfloat16 [4, 49152, 128], P('scene', 'space')
- grad_conv: float32 [3456, 128], replicated
- grad_down: float32 [1024, 256], replicated
- grad_up: float32 [256, 1024], replicated
The draws below stay inside these ranges and needn't reach their ends.
Inputs may be any that keep to these rules, and one draw needn't show every extreme that they name: The live slots of a device are its first live_count slots; on each scene some device has all 768 slots live. Only live slots have neighbours, all live and other than the slot itself. A code of 768 or more occurs only for slots below 96 (codes below 864, device s - 1 exists) or slots from 96 to 2 * 96 - 1 (codes from 864, device s + 1 exists). `destination`: among the rows of one device no owner is named more than 24 times, a bound that some block reaches. `assemble`: A permutation of the received rows of each device.
All inputs are finite; a program needn't handle non-finite values.
Results may differ from the reference program's by a relative error of at most 0.0053.
Values may be sent and summed in bfloat16 or wider, within the bound.
A program may use at most 64 MiB of HBM per device.

```python
import math
import jax
import jax.numpy as jnp
import numpy as np
from jax import lax

C = 128
CB = 256
SA = 768
RIM = 96
CAP = 24
COARSE = 192
NFINE = 49152
N_SCENE = 4
N_SPACE = 64


def brick_layout(key):
    base = jax.random.fold_in(key, 7)
    k_count, k_full, k_local, k_kind, k_rim, k_present = jax.random.split(base, 6)
    counts = jax.random.randint(k_count, (N_SCENE, N_SPACE), SA // 3, SA + 1)
    fullest = jax.random.randint(k_full, (N_SCENE,), 0, N_SPACE)
    device_ids = jnp.arange(N_SPACE, dtype=jnp.int32)
    counts = jnp.where(device_ids[None, :] == fullest[:, None], SA, counts).astype(jnp.int32)
    shape = (N_SCENE, 26, N_SPACE, SA)
    slot = jnp.arange(SA, dtype=jnp.int32)[None, None, None, :]
    device = device_ids[None, None, :, None]
    count = counts[:, None, :, None]
    present = (jax.random.randint(k_present, shape, 0, 5) < 3) & (slot < count)
    kind = jax.random.randint(k_kind, shape, 0, 3)
    local_slot = jax.random.randint(k_local, shape, 0, 1 << 20) % count
    local_slot = jnp.where(local_slot == slot, (local_slot + 1) % count, local_slot)
    rim_slot = jax.random.randint(k_rim, shape, 0, RIM)
    lower = (slot < RIM) & (device > 0) & (kind == 0)
    upper = (slot >= RIM) & (slot < 2 * RIM) & (device < N_SPACE - 1) & (kind == 0)
    target = jnp.where(lower, SA + rim_slot, jnp.where(upper, SA + RIM + rim_slot, local_slot))
    target = jnp.where(present, target, -1)
    return (counts, target.reshape(N_SCENE, 26, N_SPACE * SA).astype(jnp.int32))


def draw_live_count(key, part):
    counts, links = brick_layout(key)
    return counts


def draw_neighbours(key, part):
    counts, links = brick_layout(key)
    return links


def steps_of(rng, dims, cuts, least, largest):
    gain, own = 1.0, jax.random.fold_in(rng, 6)
    for dim, blocks in cuts:
        draws = jnp.exp(jax.random.uniform(jax.random.fold_in(own, dim), (blocks,), jnp.float32, least / len(cuts), largest / len(cuts)))
        gain = gain * jnp.repeat(draws, dims[dim] // blocks).reshape([-1 if axis == dim else 1 for axis in range(len(dims))])
    return gain


def shared_out(stream_key, own, number, rows, amount, top, reach, skew):
    ranking = jax.random.permutation(stream_key, amount)
    crowded, usual = shares(amount, rows * top, reach, skew, True), shares(amount, rows * top, reach, skew, False)
    places = jnp.arange(amount)

    def named(sizes, rotation):
        used = int((sizes > 0).sum())
        fixed = max(1, used // 4)
        shifted = fixed + (places - fixed + rotation * (used - fixed)) % max(1, amount - fixed)
        return jnp.zeros((amount,), jnp.int32).at[ranking[jnp.where(places < fixed, places, shifted)]].set(jnp.asarray(sizes, jnp.int32))

    sizes = jnp.where(number % 4 == 0, named(crowded, number // 4), named(usual, number - number // 4 - 1))
    mixed = jax.random.permutation(jax.random.fold_in(own, 3), amount)
    giver, taker = mixed[0:amount // 2 * 2:2], mixed[1:amount // 2 * 2:2]
    room = jnp.minimum(sizes[giver] - 1, reach - sizes[taker]) // 2
    room = jnp.where((giver == ranking[0]) | (taker == ranking[0]) | (sizes[taker] == 0), 0, jnp.maximum(room, 0))
    shifted = jax.random.randint(jax.random.fold_in(own, 4), (amount // 2,), 0, 1 << 20) % (room + 1)
    sizes = sizes.at[giver].add(-shifted).at[taker].add(shifted)
    items = jnp.searchsorted(jnp.cumsum(sizes), jnp.arange(rows * top), side="right").astype(jnp.int32)
    table = items.reshape(top, rows).T
    table = table[jax.random.permutation(jax.random.fold_in(own, 1), rows)]
    rotation = jax.random.randint(jax.random.fold_in(own, 2), (rows, 1), 0, top)
    return jnp.take_along_axis(table, (jnp.arange(top)[None, :] + rotation) % top, axis=1)


def shares(number_of, total, bound, lean, full):
    loads = [(1 << 20) // math.isqrt(standing ** lean) + 1 for standing in range(1, number_of + 1)]
    largest = bound if full else min(bound, max(-(-total // number_of), total * loads[0] // sum(loads)))
    least = 1 if total - largest >= number_of - 1 else 0
    given, rest = [largest] + [least] * (number_of - 1), total - largest - least * (number_of - 1)
    while rest > 0:
        movable = [i for i in range(1, number_of) if given[i] < largest] or [i for i in range(1, number_of) if given[i] < bound]
        mass, budget = sum([loads[i] for i in movable]), rest
        for i in movable:
            addition = min(bound - given[i], max(1, budget * loads[i] // mass), rest)
            given[i] = given[i] + addition
            rest = rest - addition
    return np.array(given)


def normal_values(own_key, dims, scale, reach, pieces=(), kind=jnp.bfloat16):
    entries = jax.random.normal(own_key, dims, jnp.float32) * scale
    if len(pieces) > 0:
        entries = steps_of(own_key, dims, pieces, -0.22, 0.18) * entries
    return jnp.clip(entries, min=-reach, max=reach).astype(kind)


def setup_inputs(seed: int = 0) -> dict:
    seeds = jax.random.split(jax.random.key(seed), 10)
    features = normal_values(seeds[0], (N_SCENE, NFINE, C), 1.0, 6.0, ((0, 4), (1, 64)))
    cotangent = normal_values(seeds[1], (N_SCENE, NFINE, C), (3 * (N_SCENE * N_SPACE * SA) ** -0.5), 0.09375, ((0, 4), (1, 64)))
    conv_weight = normal_values(seeds[2], (27 * C, C), (27 * C) ** -0.5, 0.109375)
    down_weight = normal_values(seeds[3], (8 * C, CB), (8 * C) ** -0.5, 0.1875)
    up_weight = normal_values(seeds[4], (CB, 8 * C), CB ** -0.5, 0.375)
    live_count = draw_live_count(jax.random.fold_in(seeds[9], 71), 0)
    neighbours = draw_neighbours(jax.random.fold_in(seeds[9], 71), 0)
    destination_keys = jax.random.split(jax.random.fold_in(seeds[7], 1), N_SCENE * NFINE // SA)
    destination_turns = jax.random.permutation(jax.random.fold_in(seeds[7], 3), N_SCENE * NFINE // SA)
    destination = jax.vmap(lambda own, number: shared_out(jax.random.fold_in(seeds[7], 2), own, number, SA, N_SPACE, 1, CAP, 1))(destination_keys, destination_turns).reshape((N_SCENE, NFINE, 1))
    assemble = jax.vmap(lambda own: jax.random.permutation(own, 2 * SA))(jax.random.split(seeds[8], N_SCENE * N_SPACE)).reshape((N_SCENE, N_SPACE, 2 * SA)).astype(jnp.int32)
    return dict(features=features, cotangent=cotangent, conv_weight=conv_weight, down_weight=down_weight, up_weight=up_weight, live_count=live_count, neighbours=neighbours, destination=destination, assemble=assemble)


def silu_grad(value):
    sigma = jax.nn.sigmoid(value)
    return sigma * (1.0 + value * (1.0 - sigma))

def route_places(dest):
    onehot = (dest[:, None] == jnp.arange(N_SPACE, dtype=jnp.int32)[None, :]).astype(jnp.int32)
    before = (jnp.cumsum(onehot, axis=0) - onehot).astype(jnp.int32)
    rank = lax.optimization_barrier(jnp.sum(before * onehot, axis=1)).astype(jnp.int32)
    return (dest * CAP + rank).astype(jnp.int32)

def reference(features, cotangent, conv_weight, down_weight, up_weight, live_count, neighbours, destination, assemble):
    outputs = []
    grad_conv = jnp.zeros((27 * C, C), jnp.float32)
    grad_down = jnp.zeros((8 * C, CB), jnp.float32)
    grad_up = jnp.zeros((CB, 8 * C), jnp.float32)
    slot_ids = jnp.arange(SA, dtype=jnp.int32)
    zero_b = jnp.zeros((), jnp.bfloat16)
    owner_dev = (jnp.arange(NFINE, dtype=jnp.int32) // SA).astype(jnp.int32)[None, :]
    for scene in range(N_SCENE):
        live = slot_ids[None, :] < live_count[scene][:, None]
        own = jnp.where(live[:, :, None], features[scene].reshape(N_SPACE, SA, C), zero_b)
        grad_rows = jnp.where(live[:, :, None], cotangent[scene].reshape(N_SPACE, SA, C), zero_b)
        table = jnp.concatenate([own.reshape(NFINE, C), jnp.zeros((1, C), jnp.bfloat16)], axis=0)
        codes = neighbours[scene]
        global_slot = jnp.where(codes < SA, owner_dev * SA + codes, jnp.where(codes < SA + RIM, (owner_dev - 1) * SA + RIM + codes - SA, (owner_dev + 1) * SA + codes - SA - RIM))
        index = jnp.where(codes < 0, NFINE, global_slot).astype(jnp.int32)

        def build(device):
            cols = lax.dynamic_slice_in_dim(index, (device * SA).astype(jnp.int32), SA, 1)
            rows = table[cols.T]
            mine = lax.dynamic_index_in_dim(own, device, 0, keepdims=False)
            return jnp.concatenate([mine[:, None, :], rows], axis=1).reshape(SA, 27 * C)

        def forward(device):
            stacked = build(device)
            pre_conv = jnp.dot(stacked, conv_weight, preferred_element_type=jnp.float32)
            return pre_conv
        devices = jnp.arange(N_SPACE, dtype=jnp.int32)
        pre_conv = lax.map(forward, devices)
        mixed = jnp.where(live[:, :, None], own.astype(jnp.float32) + jax.nn.silu(pre_conv), 0.0).astype(jnp.bfloat16)
        places = jax.vmap(route_places)(destination[scene].reshape(N_SPACE, SA))

        def pack(rows):
            sent = jax.vmap(lambda p, r: jnp.zeros((2 * SA, C), r.dtype).at[p].set(r))(places, rows)
            return sent.reshape(N_SPACE, N_SPACE, CAP, C).transpose(1, 0, 2, 3).reshape(N_SPACE, 2 * SA, C)
        order = assemble[scene]
        coarse_in = jax.vmap(lambda r, o: r[o].reshape(COARSE, 8 * C))(pack(mixed), order)
        coarse_grad = jax.vmap(lambda r, o: r[o].reshape(COARSE, 8 * C))(pack(grad_rows), order)

        def coarse_work(pair):
            x_rows, d_rows = pair
            pre = jnp.dot(x_rows, down_weight, preferred_element_type=jnp.float32)
            coarse = jax.nn.silu(pre).astype(jnp.bfloat16)
            up_rows = jnp.dot(coarse, up_weight, preferred_element_type=jnp.float32).astype(jnp.bfloat16)
            g_up = jnp.dot(coarse.T, d_rows, preferred_element_type=jnp.float32)
            back = jnp.dot(d_rows, up_weight.T, preferred_element_type=jnp.float32)
            grad_pre = (back * silu_grad(pre)).astype(jnp.bfloat16)
            g_down = jnp.dot(x_rows.T, grad_pre, preferred_element_type=jnp.float32)
            grad_in = jnp.dot(grad_pre, down_weight.T, preferred_element_type=jnp.float32).astype(jnp.bfloat16)
            return (up_rows, grad_in, g_up, g_down)
        up_rows, grad_in, g_up, g_down = lax.map(coarse_work, (coarse_in, coarse_grad))
        grad_up = grad_up + lax.optimization_barrier(jnp.sum(g_up, axis=0))
        grad_down = grad_down + lax.optimization_barrier(jnp.sum(g_down, axis=0))

        def unpack(rows):
            back_rows = jax.vmap(lambda r, o: jnp.zeros((2 * SA, C), r.dtype).at[o].set(r.reshape(2 * SA, C)))(rows, order)
            flipped = back_rows.reshape(N_SPACE, N_SPACE, CAP, C).transpose(1, 0, 2, 3).reshape(N_SPACE, 2 * SA, C)
            return jax.vmap(lambda b, p: b[p])(flipped, places)
        fine_up = unpack(up_rows)
        fine_back = unpack(grad_in)
        output = jnp.where(live[:, :, None], mixed.astype(jnp.float32) + fine_up.astype(jnp.float32), 0.0).astype(jnp.bfloat16)
        outputs.append(output.reshape(NFINE, C))
        grad_mixed = jnp.where(live[:, :, None], grad_rows.astype(jnp.float32) + fine_back.astype(jnp.float32), 0.0)
        grad_conv_pre = (grad_mixed * silu_grad(pre_conv)).astype(jnp.bfloat16)

        def conv_grad(carry, device):
            stacked = build(device)
            term = lax.dynamic_index_in_dim(grad_conv_pre, device, 0, keepdims=False)
            return (carry + jnp.dot(stacked.T, term, preferred_element_type=jnp.float32), None)
        grad_conv, unused = lax.scan(conv_grad, grad_conv, devices)
    return (jnp.stack(outputs, axis=0), grad_conv, grad_down, grad_up)
```

```python
import jax
import jax.numpy as jnp
from jax import lax
from jax.experimental import pallas as pl
from jax.experimental.pallas import tpu as pltpu
from jax.sharding import PartitionSpec as P

MESH = pl.DeviceIdType.MESH


def place():
    scene = lax.axis_index("scene")
    space = lax.axis_index("space")
    return scene, space // 8, (space // 2) % 4, space % 2


def peer(y, z, x, c):
    return {"scene": y, "space": (z * 4 + x) * 2 + c}


def reduce_kernel(
    src, out, send_c, recv_c, send_p, recv_p, send_z, recv_z, acc, sem_cs, sem_cr, sem_ps, sem_pr,
    sem_zs, sem_zr, sem_gzs, sem_gzr, sem_gps, sem_gpr, sem_gcs, sem_gcr,
):
    y, z, x, c = place()
    q = x * 4 + y
    part = src.shape[2]
    small = part // 8

    def plane(k):
        other = (q + k) % 16
        return other, peer(other % 4, z, other // 4, c)

    def column(k):
        other = (z + k) % 8
        return other, peer(y, other, x, c)

    def rows(index):
        return pl.ds(pl.multiple_of(index * small, small), small)

    partner = peer(y, z, x, 1 - c)
    barrier = pltpu.get_barrier_semaphore()
    pl.semaphore_signal(barrier, inc=1, device_id=partner, device_id_type=MESH)

    def greet_plane(k, carry):
        pl.semaphore_signal(barrier, inc=1, device_id=plane(k)[1], device_id_type=MESH)
        return carry

    def greet_column(k, carry):
        pl.semaphore_signal(barrier, inc=1, device_id=column(k)[1], device_id_type=MESH)
        return carry

    lax.fori_loop(1, 16, greet_plane, 0)
    lax.fori_loop(1, 8, greet_column, 0)
    pl.semaphore_wait(barrier, 23)

    def core_copy(k):
        return pltpu.make_async_remote_copy(
            src_ref=send_c.at[k], dst_ref=recv_c.at[k], send_sem=sem_cs.at[k], recv_sem=sem_cr.at[k],
            device_id=partner, device_id_type=MESH,
        )

    def plane_copy(k):
        return pltpu.make_async_remote_copy(
            src_ref=send_p.at[k], dst_ref=recv_p.at[k], send_sem=sem_ps.at[k], recv_sem=sem_pr.at[k],
            device_id=plane(k)[1], device_id_type=MESH,
        )

    def column_copy(k):
        return pltpu.make_async_remote_copy(
            src_ref=send_z.at[k], dst_ref=recv_z.at[k], send_sem=sem_zs.at[k], recv_sem=sem_zr.at[k],
            device_id=column(k)[1], device_id_type=MESH,
        )

    def to_core(j, carry):
        k = (j + 1) % 16
        send_c[k] = src[1 - c, plane(k)[0]].astype(jnp.bfloat16)
        core_copy(k).start()
        return carry

    lax.fori_loop(0, 16, to_core, 0)

    def to_plane(k, carry):
        core_copy(k).wait_recv()
        total = src[c, plane(k)[0]] + recv_c[k].astype(jnp.float32)
        send_p[k] = total.astype(jnp.bfloat16)
        plane_copy(k).start()
        return carry

    lax.fori_loop(1, 16, to_plane, 0)
    core_copy(0).wait_recv()
    acc[...] = src[c, q] + recv_c[0].astype(jnp.float32)

    def add_plane(k, carry):
        plane_copy(k).wait_recv()
        acc[...] += recv_p[k].astype(jnp.float32)
        return carry

    lax.fori_loop(1, 16, add_plane, 0)

    def to_column(k, carry):
        send_z[k] = acc[rows(column(k)[0]), :].astype(jnp.bfloat16)
        column_copy(k).start()
        return carry

    lax.fori_loop(1, 8, to_column, 0)

    def add_column(k, total):
        column_copy(k).wait_recv()
        return total + recv_z[k].astype(jnp.float32)

    total = lax.fori_loop(1, 8, add_column, acc[rows(z), :])
    out[c, q, rows(z), :] = total.astype(jnp.bfloat16)

    def gather_column(k, source):
        piece = out.at[c, q, rows(source), :]
        return pltpu.make_async_remote_copy(
            src_ref=piece, dst_ref=piece, send_sem=sem_gzs.at[k], recv_sem=sem_gzr.at[k],
            device_id=column(k)[1], device_id_type=MESH,
        )

    def gather_plane(k, source):
        piece = out.at[c, source]
        return pltpu.make_async_remote_copy(
            src_ref=piece, dst_ref=piece, send_sem=sem_gps.at[k], recv_sem=sem_gpr.at[k],
            device_id=plane(k)[1], device_id_type=MESH,
        )

    def gather_core(k, half):
        piece = out.at[half, (q - k + 16) % 16]
        return pltpu.make_async_remote_copy(
            src_ref=piece, dst_ref=piece, send_sem=sem_gcs.at[k], recv_sem=sem_gcr.at[k],
            device_id=partner, device_id_type=MESH,
        )

    def start_column(k, carry):
        gather_column(k, z).start()
        return carry

    def wait_column(k, carry):
        gather_column(k, (z - k + 8) % 8).wait_recv()
        return carry

    def start_plane(k, carry):
        gather_plane(k, q).start()
        return carry

    def pass_core(k, carry):
        gather_plane(k, (q - k + 16) % 16).wait_recv()
        gather_core(k, c).start()
        return carry

    lax.fori_loop(1, 8, start_column, 0)
    lax.fori_loop(1, 8, wait_column, 0)
    lax.fori_loop(1, 16, start_plane, 0)
    gather_core(0, c).start()
    lax.fori_loop(1, 16, pass_core, 0)

    def drain_core(k, carry):
        gather_core(k, 1 - c).wait_recv()
        gather_core(k, c).wait_send()
        core_copy(k).wait_send()
        return carry

    def drain_plane(k, carry):
        gather_plane(k, q).wait_send()
        plane_copy(k).wait_send()
        return carry

    def drain_column(k, carry):
        gather_column(k, z).wait_send()
        column_copy(k).wait_send()
        return carry

    lax.fori_loop(0, 16, drain_core, 0)
    lax.fori_loop(1, 16, drain_plane, 0)
    lax.fori_loop(1, 8, drain_column, 0)


def all_sum(block):
    part = block.shape[2]
    width = block.shape[3]
    dma = pltpu.SemaphoreType.DMA
    wire = jnp.bfloat16
    return pl.pallas_call(
        reduce_kernel,
        out_shape=jax.ShapeDtypeStruct(block.shape, wire),
        in_specs=[pl.BlockSpec(memory_space=pltpu.VMEM)],
        out_specs=pl.BlockSpec(memory_space=pltpu.VMEM),
        scratch_shapes=[
            pltpu.VMEM((16, part, width), wire),
            pltpu.VMEM((16, part, width), wire),
            pltpu.VMEM((16, part, width), wire),
            pltpu.VMEM((16, part, width), wire),
            pltpu.VMEM((8, part // 8, width), wire),
            pltpu.VMEM((8, part // 8, width), wire),
            pltpu.VMEM((part, width), jnp.float32),
            dma((16,)), dma((16,)), dma((16,)), dma((16,)), dma((8,)), dma((8,)),
            dma((8,)), dma((8,)), dma((16,)), dma((16,)), dma((16,)), dma((16,)),
        ],
        compiler_params=pltpu.CompilerParams(collective_id=0, has_side_effects=True),
        name="sum_gradients",
    )(block)


def extended(block, sides, width):
    for axis, dim in sides:
        count = lax.axis_size(axis)
        forward = [(i, i + 1) for i in range(count - 1)]
        backward = [(target, source) for source, target in forward]
        low = lax.ppermute(
            lax.slice_in_dim(block, block.shape[dim] - width, None, axis=dim), axis, forward
        )
        high = lax.ppermute(lax.slice_in_dim(block, 0, width, axis=dim), axis, backward)
        block = jnp.concatenate([low, block, high], axis=dim)
    return block


def silu_grad(value):
    sigma = jax.nn.sigmoid(value)
    return sigma * (1.0 + value * (1.0 - sigma))


def contract_rows(left, right):
    return lax.dot_general(
        left, right, (((0,), (0,)), ((), ())), preferred_element_type=jnp.float32
    )


def contract_cols(left, right):
    return lax.dot_general(
        left, right, (((1,), (1,)), ((), ())), preferred_element_type=jnp.float32
    )


def on_device(
    features,
    cotangent,
    conv_weight,
    down_weight,
    up_weight,
    live_count,
    neighbours,
    destination,
    assemble,
):
    slots = features.shape[1]
    width = features.shape[2]
    places = lax.axis_size("space")
    rim = slots // 8
    cap = 2 * slots // places
    zero_b = jnp.zeros((), jnp.bfloat16)
    live = (jnp.arange(slots, dtype=jnp.int32) < live_count[0, 0])[:, None]
    own = jnp.where(live, features[0], zero_b)
    grad_rows = jnp.where(live, cotangent[0], zero_b)
    dest = destination[0, :, 0]
    onehot = (dest[:, None] == jnp.arange(places, dtype=jnp.int32)[None, :]).astype(jnp.int32)
    rank = jnp.sum((jnp.cumsum(onehot, axis=0) - onehot) * onehot, axis=1)
    target = dest * cap + rank

    def pack(rows):
        return (
            jnp.zeros((2 * slots, width), rows.dtype)
            .at[target]
            .set(rows)
            .reshape(places, cap, width)
        )

    codes = neighbours[0].T
    zero_row = jnp.zeros((1, width), jnp.bfloat16)
    padded = extended(own[None], (("space", 0),), 1)
    table = jnp.concatenate([padded.reshape(3 * slots, width), zero_row], axis=0)
    index = jnp.where(
        codes < slots,
        slots + codes,
        jnp.where(codes < slots + rim, rim + codes - slots, 2 * slots + codes - slots - rim),
    )
    index = jnp.where(codes < 0, 3 * slots, index)
    rows = table[index]
    stacked = jnp.concatenate([own[:, None, :], rows], axis=1).reshape(slots, 27 * width)
    pre_conv = jnp.dot(stacked, conv_weight, preferred_element_type=jnp.float32)
    mixed = jnp.where(live, own.astype(jnp.float32) + jax.nn.silu(pre_conv), 0.0).astype(
        jnp.bfloat16
    )
    stacked, pre_conv, mixed = (stacked, pre_conv, mixed)
    got_mixed, got_grad = (
        lax.all_to_all(pack(mixed), "space", split_axis=0, concat_axis=0, tiled=True),
        lax.all_to_all(pack(grad_rows), "space", split_axis=0, concat_axis=0, tiled=True),
    )
    order = assemble[0, 0]
    coarse_rows = 2 * slots // 8
    coarse_in = got_mixed.reshape(2 * slots, width)[order].reshape(coarse_rows, 8 * width)
    coarse_grad = got_grad.reshape(2 * slots, width)[order].reshape(coarse_rows, 8 * width)
    pre = jnp.dot(coarse_in, down_weight, preferred_element_type=jnp.float32)
    coarse = jax.nn.silu(pre).astype(jnp.bfloat16)
    up_rows = jnp.dot(coarse, up_weight, preferred_element_type=jnp.float32).astype(jnp.bfloat16)
    grad_up = contract_rows(coarse, coarse_grad)
    back = contract_cols(coarse_grad, up_weight)
    grad_pre = (back * silu_grad(pre)).astype(jnp.bfloat16)
    grad_down = contract_rows(coarse_in, grad_pre)
    grad_in = contract_cols(grad_pre, down_weight).astype(jnp.bfloat16)

    def unpack(rows):
        return (
            jnp.zeros((2 * slots, width), jnp.bfloat16)
            .at[order]
            .set(rows.reshape(2 * slots, width))
            .reshape(places, cap, width)
        )

    got_up, got_back = (
        lax.all_to_all(unpack(up_rows), "space", split_axis=0, concat_axis=0, tiled=True),
        lax.all_to_all(unpack(grad_in), "space", split_axis=0, concat_axis=0, tiled=True),
    )
    fine_up = got_up.reshape(2 * slots, width)[target]
    fine_back = got_back.reshape(2 * slots, width)[target]
    output = jnp.where(live, mixed.astype(jnp.float32) + fine_up.astype(jnp.float32), 0.0).astype(
        jnp.bfloat16
    )
    grad_mixed = jnp.where(live, grad_rows.astype(jnp.float32) + fine_back.astype(jnp.float32), 0.0)
    grad_conv_pre = (grad_mixed * silu_grad(pre_conv)).astype(jnp.bfloat16)
    grad_conv = contract_rows(stacked, grad_conv_pre)
    taps, wide = grad_conv.shape[0], grad_up.shape[0]
    deep = grad_down.shape[0]
    spare = jnp.zeros((deep * 4 - taps, width), jnp.float32)
    down = grad_down.reshape(deep, wide // width, width).transpose(1, 0, 2).reshape(-1, width)
    up = grad_up.reshape(wide, deep // width, width).transpose(1, 0, 2).reshape(-1, width)
    block = jnp.concatenate([grad_conv, spare, down, up], axis=0)
    total = all_sum(block.reshape(2, 16, -1, width)).reshape(-1, width)
    grad_conv = total[:taps].astype(jnp.float32)
    down = total[deep * 4 : deep * 4 + down.shape[0]].reshape(wide // width, deep, width)
    up = total[deep * 4 + down.shape[0] * down.shape[1] :].reshape(deep // width, wide, width)
    grad_down = down.transpose(1, 0, 2).reshape(deep, wide).astype(jnp.float32)
    grad_up = up.transpose(1, 0, 2).reshape(wide, deep).astype(jnp.float32)
    return (output[None], grad_conv, grad_down, grad_up)


def solution(mesh):
    in_specs = (
        P("scene", "space", None),
        P("scene", "space", None),
        P(),
        P(),
        P(),
        P("scene", "space"),
        P("scene", None, "space"),
        P("scene", "space", None),
        P("scene", "space", None),
    )
    out_specs = (P("scene", "space", None), P(), P(), P())
    return jax.shard_map(
        on_device, mesh=mesh, in_specs=in_specs, out_specs=out_specs, check_vma=False
    )
```

```python
import jax
import jax.numpy as jnp
from jax import lax
from jax.experimental import pallas as pl
from jax.experimental.pallas import tpu as pltpu
from jax.sharding import PartitionSpec as P

def silu_grad(value):
    sigma = jax.nn.sigmoid(value)
    return sigma * (1.0 + value * (1.0 - sigma))


MESH = pl.DeviceIdType.MESH


def place():
    scene = lax.axis_index("scene")
    space = lax.axis_index("space")
    return scene, space // 8, (space // 2) % 4, space % 2


def peer(y, z, x, c):
    return {"scene": y, "space": (z * 4 + x) * 2 + c}


def reduce_kernel(
    src, out, send_c, recv_c, send_p, recv_p, send_z, recv_z, acc, sem_cs, sem_cr, sem_ps, sem_pr,
    sem_zs, sem_zr, sem_gzs, sem_gzr, sem_gps, sem_gpr, sem_gcs, sem_gcr,
):
    y, z, x, c = place()
    q = x * 4 + y
    part = src.shape[2]
    small = part // 8

    def plane(k):
        other = (q + k) % 16
        return other, peer(other % 4, z, other // 4, c)

    def column(k):
        other = (z + k) % 8
        return other, peer(y, other, x, c)

    def rows(index):
        return pl.ds(pl.multiple_of(index * small, small), small)

    partner = peer(y, z, x, 1 - c)
    barrier = pltpu.get_barrier_semaphore()
    pl.semaphore_signal(barrier, inc=1, device_id=partner, device_id_type=MESH)

    def greet_plane(k, carry):
        pl.semaphore_signal(barrier, inc=1, device_id=plane(k)[1], device_id_type=MESH)
        return carry

    def greet_column(k, carry):
        pl.semaphore_signal(barrier, inc=1, device_id=column(k)[1], device_id_type=MESH)
        return carry

    lax.fori_loop(1, 16, greet_plane, 0)
    lax.fori_loop(1, 8, greet_column, 0)
    pl.semaphore_wait(barrier, 23)

    def core_copy(k):
        return pltpu.make_async_remote_copy(
            src_ref=send_c.at[k], dst_ref=recv_c.at[k], send_sem=sem_cs.at[k], recv_sem=sem_cr.at[k],
            device_id=partner, device_id_type=MESH,
        )

    def plane_copy(k):
        return pltpu.make_async_remote_copy(
            src_ref=send_p.at[k], dst_ref=recv_p.at[k], send_sem=sem_ps.at[k], recv_sem=sem_pr.at[k],
            device_id=plane(k)[1], device_id_type=MESH,
        )

    def column_copy(k):
        return pltpu.make_async_remote_copy(
            src_ref=send_z.at[k], dst_ref=recv_z.at[k], send_sem=sem_zs.at[k], recv_sem=sem_zr.at[k],
            device_id=column(k)[1], device_id_type=MESH,
        )

    def to_core(j, carry):
        k = (j + 1) % 16
        send_c[k] = src[1 - c, plane(k)[0]].astype(jnp.bfloat16)
        core_copy(k).start()
        return carry

    lax.fori_loop(0, 16, to_core, 0)

    def to_plane(k, carry):
        core_copy(k).wait_recv()
        total = src[c, plane(k)[0]] + recv_c[k].astype(jnp.float32)
        send_p[k] = total.astype(jnp.bfloat16)
        plane_copy(k).start()
        return carry

    lax.fori_loop(1, 16, to_plane, 0)
    core_copy(0).wait_recv()
    acc[...] = src[c, q] + recv_c[0].astype(jnp.float32)

    def add_plane(k, carry):
        plane_copy(k).wait_recv()
        acc[...] += recv_p[k].astype(jnp.float32)
        return carry

    lax.fori_loop(1, 16, add_plane, 0)

    def to_column(k, carry):
        send_z[k] = acc[rows(column(k)[0]), :].astype(jnp.bfloat16)
        column_copy(k).start()
        return carry

    lax.fori_loop(1, 8, to_column, 0)

    def add_column(k, total):
        column_copy(k).wait_recv()
        return total + recv_z[k].astype(jnp.float32)

    total = lax.fori_loop(1, 8, add_column, acc[rows(z), :])
    out[c, q, rows(z), :] = total.astype(jnp.bfloat16)

    def gather_column(k, source):
        piece = out.at[c, q, rows(source), :]
        return pltpu.make_async_remote_copy(
            src_ref=piece, dst_ref=piece, send_sem=sem_gzs.at[k], recv_sem=sem_gzr.at[k],
            device_id=column(k)[1], device_id_type=MESH,
        )

    def gather_plane(k, source):
        piece = out.at[c, source]
        return pltpu.make_async_remote_copy(
            src_ref=piece, dst_ref=piece, send_sem=sem_gps.at[k], recv_sem=sem_gpr.at[k],
            device_id=plane(k)[1], device_id_type=MESH,
        )

    def gather_core(k, half):
        piece = out.at[half, (q - k + 16) % 16]
        return pltpu.make_async_remote_copy(
            src_ref=piece, dst_ref=piece, send_sem=sem_gcs.at[k], recv_sem=sem_gcr.at[k],
            device_id=partner, device_id_type=MESH,
        )

    def start_column(k, carry):
        gather_column(k, z).start()
        return carry

    def wait_column(k, carry):
        gather_column(k, (z - k + 8) % 8).wait_recv()
        return carry

    def start_plane(k, carry):
        gather_plane(k, q).start()
        return carry

    def pass_core(k, carry):
        gather_plane(k, (q - k + 16) % 16).wait_recv()
        gather_core(k, c).start()
        return carry

    lax.fori_loop(1, 8, start_column, 0)
    lax.fori_loop(1, 8, wait_column, 0)
    lax.fori_loop(1, 16, start_plane, 0)
    gather_core(0, c).start()
    lax.fori_loop(1, 16, pass_core, 0)

    def drain_core(k, carry):
        gather_core(k, 1 - c).wait_recv()
        gather_core(k, c).wait_send()
        core_copy(k).wait_send()
        return carry

    def drain_plane(k, carry):
        gather_plane(k, q).wait_send()
        plane_copy(k).wait_send()
        return carry

    def drain_column(k, carry):
        gather_column(k, z).wait_send()
        column_copy(k).wait_send()
        return carry

    lax.fori_loop(0, 16, drain_core, 0)
    lax.fori_loop(1, 16, drain_plane, 0)
    lax.fori_loop(1, 8, drain_column, 0)


def all_sum(block):
    part = block.shape[2]
    width = block.shape[3]
    dma = pltpu.SemaphoreType.DMA
    wire = jnp.bfloat16
    return pl.pallas_call(
        reduce_kernel,
        out_shape=jax.ShapeDtypeStruct(block.shape, wire),
        in_specs=[pl.BlockSpec(memory_space=pltpu.VMEM)],
        out_specs=pl.BlockSpec(memory_space=pltpu.VMEM),
        scratch_shapes=[
            pltpu.VMEM((16, part, width), wire),
            pltpu.VMEM((16, part, width), wire),
            pltpu.VMEM((16, part, width), wire),
            pltpu.VMEM((16, part, width), wire),
            pltpu.VMEM((8, part // 8, width), wire),
            pltpu.VMEM((8, part // 8, width), wire),
            pltpu.VMEM((part, width), jnp.float32),
            dma((16,)), dma((16,)), dma((16,)), dma((16,)), dma((8,)), dma((8,)),
            dma((8,)), dma((8,)), dma((16,)), dma((16,)), dma((16,)), dma((16,)),
        ],
        compiler_params=pltpu.CompilerParams(collective_id=0, has_side_effects=True),
        name="sum_gradients",
    )(block)


def one_hot(condition):
    return jnp.where(condition, 1.0, 0.0).astype(jnp.bfloat16)


def iota(shape, axis):
    return lax.broadcasted_iota(jnp.int32, shape, axis)


def dot(left, right, left_axis=1, right_axis=0):
    return lax.dot_general(
        left, right, (((left_axis,), (right_axis,)), ((), ())), preferred_element_type=jnp.float32
    )


def step_kernel(
    features, cotangent, conv_weight, down_weight, up_weight, live_count, codes, dest, order,
    output, block,
    own, grads, table, weight_t, stacked, pre_fine, mixed, rim, target_row, target_col, order_col,
    send_m, recv_m, send_g, recv_g, send_u, recv_u, joined, coarse_in, coarse_grad, returned, slope,
    sem_rs, sem_rr, sem_ms, sem_mr, sem_gs, sem_gr, sem_us, sem_ur,
):
    y, z, x, c = place()
    me = (z * 4 + x) * 2 + c
    slots, width = features.shape
    edge = slots // 8
    places, cap = send_m.shape[0], send_m.shape[1]
    group = 8
    span = group * cap
    bricks = coarse_in.shape[0]
    taps = codes.shape[0]

    def at(device):
        return {"scene": y, "space": device}

    rim[...] = jnp.zeros_like(rim)
    barrier = pltpu.get_barrier_semaphore()

    def greet(k, carry):
        pl.semaphore_signal(
            barrier, inc=1, device_id=at((me + k) % places), device_id_type=MESH
        )
        return carry

    lax.fori_loop(1, places, greet, 0)

    count = live_count[0, 0]
    live = iota((slots, width), 0) < count
    zero_b = jnp.zeros((slots, width), jnp.bfloat16)
    own[...] = jnp.where(live, features[...], zero_b)
    grads[...] = jnp.where(live, cotangent[...], zero_b)

    goal = dest[...]
    named = goal == iota((places, slots), 0)
    named_b = one_hot(named)
    for part in range(3):
        cols = slice(part * 256, part * 256 + 256)
        earlier = one_hot(iota((slots, 256), 0) < iota((slots, 256), 1) + part * 256)
        before = dot(named_b, earlier)
        rank = jnp.sum(jnp.where(named[:, cols], before, 0.0), axis=0, keepdims=True)
        row = goal[:, cols].astype(jnp.float32) * cap + rank
        target_row[:, cols] = row
        target_col[cols, :] = jnp.broadcast_to(row, (128, 256)).T

    for part in range(12):
        cols = slice(part * 128, part * 128 + 128)
        order_col[cols, :] = jnp.broadcast_to(order[:, cols].astype(jnp.float32), (128, 128)).T

    pl.semaphore_wait(barrier, places - 1)

    def rim_copy(upward):
        start = edge if upward else 0
        there = 0 if upward else edge
        return pltpu.make_async_remote_copy(
            src_ref=features.at[pl.ds(start, edge), :], dst_ref=rim.at[pl.ds(there, edge), :],
            send_sem=sem_rs.at[1 - int(upward)], recv_sem=sem_rr.at[1 - int(upward)],
            device_id=at((me + (1 if upward else places - 1)) % places), device_id_type=MESH,
        )

    @pl.when(me < places - 1)
    def _():
        rim_copy(True).start()

    @pl.when(me > 0)
    def _():
        rim_copy(False).start()

    def exchange(sent, received, send_sems, recv_sems, device, source):
        return pltpu.make_async_remote_copy(
            src_ref=sent.at[device], dst_ref=received.at[source],
            send_sem=send_sems.at[device], recv_sem=recv_sems.at[source],
            device_id=at(device), device_id_type=MESH,
        )

    def send_group(which, sent, received, send_sems, recv_sems):
        def one(k, carry):
            device = which * group + (me + k) % group

            @pl.when(device != me)
            def _():
                exchange(sent, received, send_sems, recv_sems, device, me).start()

            return carry

        lax.fori_loop(0, group, one, 0)

    def in_order(j):
        odd = j % 2
        return (z + 4 - odd + (1 - 2 * odd) * (j // 2)) % 8

    def spread(rows, sent, received, send_sems, recv_sems):
        def one(j, carry):
            which = in_order(j)
            chosen = one_hot(
                (iota((span, slots), 0) + which * span).astype(jnp.float32) == target_row[...]
            )
            packed = dot(chosen, rows[...]).reshape(group, cap, width).astype(jnp.bfloat16)
            sent[pl.ds(which * group, group)] = packed
            send_group(which, sent, received, send_sems, recv_sems)
            return carry

        lax.fori_loop(0, places // group, one, 0)
        received[pl.ds(me, 1)] = sent[pl.ds(me, 1)]

    spread(grads, send_g, recv_g, sem_gs, sem_gr)

    def turn(k, carry):
        rows = pl.ds(pl.multiple_of(k * width, width), width)
        weight_t[:, rows] = conv_weight[rows, :].astype(jnp.float32).T.astype(jnp.bfloat16)
        return carry

    lax.fori_loop(0, taps + 1, turn, 0)
    for part in range(6):
        cols = slice(part * 128, part * 128 + 128)
        turned = own[cols, :].astype(jnp.float32).T.astype(jnp.bfloat16)
        table[:, cols] = turned
        stacked[0:width, cols] = turned

    def pick(k, part, depth):
        code = codes[pl.ds(k, 1), part * 256 : part * 256 + 256]
        chosen = one_hot(iota((depth, 256), 0) == code)
        found = dot(table[:, 0:depth], chosen).astype(jnp.bfloat16)
        rows = pl.ds(pl.multiple_of((k + 1) * width, width), width)
        stacked[rows, part * 256 : part * 256 + 256] = found

    def inner(k, carry):
        pick(k, 1, slots)
        pick(k, 2, slots)
        return carry

    lax.fori_loop(0, taps, inner, 0)

    @pl.when(me > 0)
    def _():
        rim_copy(True).wait_recv()

    @pl.when(me < places - 1)
    def _():
        rim_copy(False).wait_recv()

    table[:, slots:] = rim[...].astype(jnp.float32).T.astype(jnp.bfloat16)

    def outer(k, carry):
        pick(k, 0, slots + 256)
        return carry

    lax.fori_loop(0, taps, outer, 0)

    for part in range(3):
        cols = slice(part * 256, part * 256 + 256)
        pre = dot(weight_t[...], stacked[:, cols]).T
        pre_fine[cols, :] = pre
        alive = iota((256, width), 0) + part * 256 < count
        blend = jnp.where(alive, own[cols, :].astype(jnp.float32) + jax.nn.silu(pre), 0.0)
        mixed[cols, :] = blend.astype(jnp.bfloat16)

    spread(mixed, send_m, recv_m, sem_ms, sem_mr)

    def arrived(received, sent, send_sems, recv_sems):
        def one(k, carry):
            exchange(sent, received, send_sems, recv_sems, me, (me + k) % places).wait_recv()
            return carry

        lax.fori_loop(1, places, one, 0)

    def left(received, sent, send_sems, recv_sems):
        def one(k, carry):
            exchange(sent, received, send_sems, recv_sems, (me + k) % places, me).wait_send()
            return carry

        lax.fori_loop(1, places, one, 0)

    def flat(received, lanes, base):
        def one(j, carry):
            rows = pl.ds(pl.multiple_of(j * span, span), span)
            value = received[pl.ds(j * group, group)].astype(jnp.float32)
            joined[rows, base : base + lanes] = value.reshape(span, lanes).astype(jnp.bfloat16)
            return carry

        lax.fori_loop(0, places // group, one, 0)

    arrived(recv_g, send_g, sem_gs, sem_gr)
    flat(recv_g, width, width)
    arrived(recv_m, send_m, sem_ms, sem_mr)
    flat(recv_m, width, 0)

    received_rows = places * cap

    def bring(k, carry):
        rows = pl.ds(pl.multiple_of(k * bricks, bricks), bricks)
        cols = pl.ds(pl.multiple_of(k * width, width), width)
        chosen = one_hot(
            order_col[rows, 0:1] == iota((bricks, received_rows), 1).astype(jnp.float32)
        )
        pair = dot(chosen, joined[...]).astype(jnp.bfloat16)
        coarse_in[:, cols] = pair[:, 0:width]
        coarse_grad[:, cols] = pair[:, width:]
        return carry

    lax.fori_loop(0, 8, bring, 0)

    pre = dot(coarse_in[...], down_weight[...])
    coarse = jax.nn.silu(pre).astype(jnp.bfloat16)
    back = dot(coarse_grad[...], up_weight[...], 1, 1)
    grad_pre = (back * silu_grad(pre)).astype(jnp.bfloat16)
    up_rows = dot(coarse, up_weight[...]).astype(jnp.bfloat16)
    grad_in = dot(grad_pre, down_weight[...], 1, 1).astype(jnp.bfloat16)
    for k in range(8):
        rows = slice(k * bricks, k * bricks + bricks)
        returned[rows, 0:width] = up_rows[:, k * width : k * width + width]
        returned[rows, width:] = grad_in[:, k * width : k * width + width]

    def give(j, carry):
        which = in_order(j)
        chosen = one_hot(iota((span, received_rows), 0) + which * span == order[...])
        packed = dot(chosen, returned[...]).reshape(group, cap, 2 * width).astype(jnp.bfloat16)
        send_u[pl.ds(which * group, group)] = packed
        send_group(which, send_u, recv_u, sem_us, sem_ur)
        return carry

    lax.fori_loop(0, places // group, give, 0)
    recv_u[pl.ds(me, 1)] = send_u[pl.ds(me, 1)]

    deep, wide = down_weight.shape
    base = 4 * deep
    grad_down = dot(coarse_in[...], grad_pre, 0, 0)
    for k in range(wide // width):
        block[base + k * deep : base + (k + 1) * deep, :] = grad_down[:, k * width : k * width + width]
    base = base + deep * wide // width
    grad_up = dot(coarse, coarse_grad[...], 0, 0)
    for k in range(deep // width):
        block[base + k * wide : base + (k + 1) * wide, :] = grad_up[:, k * width : k * width + width]

    arrived(recv_u, send_u, sem_us, sem_ur)
    flat(recv_u, 2 * width, 0)

    def settle(part, carry):
        rows = pl.ds(pl.multiple_of(part * 256, 256), 256)
        chosen = one_hot(
            target_col[rows, 0:1] == iota((256, received_rows), 1).astype(jnp.float32)
        )
        fine = dot(chosen, joined[...])
        alive = iota((256, width), 0) + part * 256 < count
        total = mixed[rows, :].astype(jnp.float32) + fine[:, 0:width]
        output[rows, :] = jnp.where(alive, total, 0.0).astype(jnp.bfloat16)
        grad_mixed = jnp.where(alive, grads[rows, :].astype(jnp.float32) + fine[:, width:], 0.0)
        slope[rows, :] = (grad_mixed * silu_grad(pre_fine[rows, :])).astype(jnp.bfloat16)
        return carry

    lax.fori_loop(0, 3, settle, 0)

    def convolve(k, carry):
        rows = pl.ds(pl.multiple_of(k * 384, 384), 384)
        block[rows, :] = dot(stacked[rows, :], slope[...])
        return carry

    lax.fori_loop(0, 9, convolve, 0)
    block[27 * width : 4 * deep, :] = jnp.zeros((4 * deep - 27 * width, width), jnp.float32)

    left(recv_g, send_g, sem_gs, sem_gr)
    left(recv_m, send_m, sem_ms, sem_mr)
    left(recv_u, send_u, sem_us, sem_ur)

    @pl.when(me < places - 1)
    def _():
        rim_copy(True).wait_send()

    @pl.when(me > 0)
    def _():
        rim_copy(False).wait_send()


def whole_step(features, cotangent, conv_weight, down_weight, up_weight, live_count, codes, dest, order):
    slots, width = features.shape
    taps = codes.shape[0]
    deep, wide = down_weight.shape
    rows = order.shape[1]
    places = lax.axis_size("space")
    cap = rows // places
    bricks = rows // 8
    wire = jnp.bfloat16
    dma = pltpu.SemaphoreType.DMA
    vmem = pl.BlockSpec(memory_space=pltpu.VMEM)
    smem = pl.BlockSpec(memory_space=pltpu.SMEM)
    return pl.pallas_call(
        step_kernel,
        out_shape=(
            jax.ShapeDtypeStruct((slots, width), wire),
            jax.ShapeDtypeStruct((8 * deep, width), jnp.float32),
        ),
        in_specs=[vmem, vmem, vmem, vmem, vmem, smem, vmem, vmem, vmem],
        out_specs=(vmem, vmem),
        scratch_shapes=[
            pltpu.VMEM((slots, width), wire),
            pltpu.VMEM((slots, width), wire),
            pltpu.VMEM((width, slots + 256), wire),
            pltpu.VMEM((width, (taps + 1) * width), wire),
            pltpu.VMEM(((taps + 1) * width, slots), wire),
            pltpu.VMEM((slots, width), jnp.float32),
            pltpu.VMEM((slots, width), wire),
            pltpu.VMEM((256, width), wire),
            pltpu.VMEM((1, slots), jnp.float32),
            pltpu.VMEM((slots, 128), jnp.float32),
            pltpu.VMEM((rows, 128), jnp.float32),
            pltpu.VMEM((places, cap, width), wire),
            pltpu.VMEM((places, cap, width), wire),
            pltpu.VMEM((places, cap, width), wire),
            pltpu.VMEM((places, cap, width), wire),
            pltpu.VMEM((places, cap, 2 * width), wire),
            pltpu.VMEM((places, cap, 2 * width), wire),
            pltpu.VMEM((rows, 2 * width), wire),
            pltpu.VMEM((bricks, deep), wire),
            pltpu.VMEM((bricks, deep), wire),
            pltpu.VMEM((rows, 2 * width), wire),
            pltpu.VMEM((slots, width), wire),
            dma((2,)), dma((2,)), dma((places,)), dma((places,)), dma((places,)), dma((places,)),
            dma((places,)), dma((places,)),
        ],
        compiler_params=pltpu.CompilerParams(collective_id=1, has_side_effects=True),
        name="brick_step",
    )(features, cotangent, conv_weight, down_weight, up_weight, live_count, codes, dest, order)


def on_device(
    features, cotangent, conv_weight, down_weight, up_weight, live_count, neighbours, destination, assemble
):
    slots, width = features.shape[1], features.shape[2]
    deep, wide = down_weight.shape
    taps = conv_weight.shape[0]
    order = assemble[0, 0].reshape(-1, 8).T.reshape(1, -1)
    output, block = whole_step(
        features[0], cotangent[0], conv_weight, down_weight, up_weight, live_count,
        neighbours[0], destination[0].reshape(1, slots), order,
    )
    total = all_sum(block.reshape(2, 16, -1, width)).reshape(-1, width)
    grad_conv = total[:taps].astype(jnp.float32)
    half = deep * wide // width
    down = total[deep * 4 : deep * 4 + half].reshape(wide // width, deep, width)
    up = total[deep * 4 + half :].reshape(deep // width, wide, width)
    grad_down = down.transpose(1, 0, 2).reshape(deep, wide).astype(jnp.float32)
    grad_up = up.transpose(1, 0, 2).reshape(wide, deep).astype(jnp.float32)
    return (output[None], grad_conv, grad_down, grad_up)


def solution(mesh):
    in_specs = (
        P("scene", "space", None),
        P("scene", "space", None),
        P(),
        P(),
        P(),
        P("scene", "space"),
        P("scene", None, "space"),
        P("scene", "space", None),
        P("scene", "space", None),
    )
    out_specs = (P("scene", "space", None), P(), P(), P())
    return jax.shard_map(
        on_device, mesh=mesh, in_specs=in_specs, out_specs=out_specs, check_vma=False
    )
```

```python
import jax
import jax.numpy as jnp
from jax import lax
from jax.experimental import pallas as pl
from jax.experimental.pallas import tpu as pltpu
from jax.sharding import PartitionSpec as P

def silu_grad(value):
    sigma = jax.nn.sigmoid(value)
    return sigma * (1.0 + value * (1.0 - sigma))


MESH = pl.DeviceIdType.MESH


def place():
    scene = lax.axis_index("scene")
    space = lax.axis_index("space")
    return scene, space // 8, (space // 2) % 4, space % 2


def peer(y, z, x, c):
    return {"scene": y, "space": (z * 4 + x) * 2 + c}


def reducer(
    src, out, send_c, recv_c, send_p, recv_p, send_z, recv_z, acc, sem_cs, sem_cr, sem_ps, sem_pr,
    sem_zs, sem_zr, sem_gzs, sem_gzr, sem_gps, sem_gpr, sem_gcs, sem_gcr,
):
    y, z, x, c = place()
    q = x * 4 + y
    part, width = acc.shape
    small = part // 8

    def local(half, index):
        return src[pl.ds(pl.multiple_of((half * 16 + index) * part, part), part), :]

    def plane(k):
        other = (q + k) % 16
        return other, peer(other % 4, z, other // 4, c)

    def column(k):
        other = (z + k) % 8
        return other, peer(y, other, x, c)

    def rows(index):
        return pl.ds(pl.multiple_of(index * small, small), small)

    partner = peer(y, z, x, 1 - c)

    def greet(barrier):
        pl.semaphore_signal(barrier, inc=1, device_id=partner, device_id_type=MESH)

        def greet_plane(k, carry):
            pl.semaphore_signal(barrier, inc=1, device_id=plane(k)[1], device_id_type=MESH)
            return carry

        def greet_column(k, carry):
            pl.semaphore_signal(barrier, inc=1, device_id=column(k)[1], device_id_type=MESH)
            return carry

        lax.fori_loop(1, 16, greet_plane, 0)
        lax.fori_loop(1, 8, greet_column, 0)

    def core_copy(k):
        return pltpu.make_async_remote_copy(
            src_ref=send_c.at[k], dst_ref=recv_c.at[k], send_sem=sem_cs.at[k], recv_sem=sem_cr.at[k],
            device_id=partner, device_id_type=MESH,
        )

    def plane_copy(k):
        return pltpu.make_async_remote_copy(
            src_ref=send_p.at[k], dst_ref=recv_p.at[k], send_sem=sem_ps.at[k], recv_sem=sem_pr.at[k],
            device_id=plane(k)[1], device_id_type=MESH,
        )

    def column_copy(k):
        return pltpu.make_async_remote_copy(
            src_ref=send_z.at[k], dst_ref=recv_z.at[k], send_sem=sem_zs.at[k], recv_sem=sem_zr.at[k],
            device_id=column(k)[1], device_id_type=MESH,
        )

    def to_core(j, carry):
        k = (j + 1) % 16
        send_c[k] = local(1 - c, plane(k)[0]).astype(jnp.bfloat16)
        core_copy(k).start()
        return carry

    def to_plane(k, carry):
        core_copy(k).wait_recv()
        total = local(c, plane(k)[0]) + recv_c[k].astype(jnp.float32)
        send_p[k] = total.astype(jnp.bfloat16)
        plane_copy(k).start()
        return carry

    def begin():
        @pl.when(c == 0)
        def _():
            lax.fori_loop(0, 16, to_core, 0)

        @pl.when(c == 1)
        def _():
            lax.fori_loop(1, 16, to_plane, 0)

    def finish():
        @pl.when(c == 1)
        def _():
            lax.fori_loop(0, 16, to_core, 0)

        @pl.when(c == 0)
        def _():
            lax.fori_loop(1, 16, to_plane, 0)

        core_copy(0).wait_recv()
        acc[...] = local(c, q) + recv_c[0].astype(jnp.float32)

        def add_plane(k, carry):
            plane_copy(k).wait_recv()
            acc[...] += recv_p[k].astype(jnp.float32)
            return carry

        lax.fori_loop(1, 16, add_plane, 0)

        def to_column(k, carry):
            send_z[k] = acc[rows(column(k)[0]), :].astype(jnp.bfloat16)
            column_copy(k).start()
            return carry

        lax.fori_loop(1, 8, to_column, 0)

        def add_column(k, total):
            column_copy(k).wait_recv()
            return total + recv_z[k].astype(jnp.float32)

        total = lax.fori_loop(1, 8, add_column, acc[rows(z), :])
        out[c, q, rows(z), :] = total.astype(jnp.bfloat16)

        def gather_column(k, source):
            piece = out.at[c, q, rows(source), :]
            return pltpu.make_async_remote_copy(
                src_ref=piece, dst_ref=piece, send_sem=sem_gzs.at[k], recv_sem=sem_gzr.at[k],
                device_id=column(k)[1], device_id_type=MESH,
            )

        def gather_plane(k, source):
            piece = out.at[c, source]
            return pltpu.make_async_remote_copy(
                src_ref=piece, dst_ref=piece, send_sem=sem_gps.at[k], recv_sem=sem_gpr.at[k],
                device_id=plane(k)[1], device_id_type=MESH,
            )

        def gather_core(k, half):
            piece = out.at[half, (q - k + 16) % 16]
            return pltpu.make_async_remote_copy(
                src_ref=piece, dst_ref=piece, send_sem=sem_gcs.at[k], recv_sem=sem_gcr.at[k],
                device_id=partner, device_id_type=MESH,
            )

        def start_column(k, carry):
            gather_column(k, z).start()
            return carry

        def wait_column(k, carry):
            gather_column(k, (z - k + 8) % 8).wait_recv()
            return carry

        def start_plane(k, carry):
            gather_plane(k, q).start()
            return carry

        def pass_core(k, carry):
            gather_plane(k, (q - k + 16) % 16).wait_recv()
            gather_core(k, c).start()
            return carry

        lax.fori_loop(1, 8, start_column, 0)
        lax.fori_loop(1, 8, wait_column, 0)
        lax.fori_loop(1, 16, start_plane, 0)
        gather_core(0, c).start()
        lax.fori_loop(1, 16, pass_core, 0)

        def drain_core(k, carry):
            gather_core(k, 1 - c).wait_recv()
            gather_core(k, c).wait_send()
            core_copy(k).wait_send()
            return carry

        def drain_plane(k, carry):
            gather_plane(k, q).wait_send()
            plane_copy(k).wait_send()
            return carry

        def drain_column(k, carry):
            gather_column(k, z).wait_send()
            column_copy(k).wait_send()
            return carry

        lax.fori_loop(0, 16, drain_core, 0)
        lax.fori_loop(1, 16, drain_plane, 0)
        lax.fori_loop(1, 8, drain_column, 0)

    return greet, begin, finish


def one_hot(condition):
    return jnp.where(condition, 1.0, 0.0).astype(jnp.bfloat16)


def iota(shape, axis):
    return lax.broadcasted_iota(jnp.int32, shape, axis)


def dot(left, right, left_axis=1, right_axis=0):
    return lax.dot_general(
        left, right, (((left_axis,), (right_axis,)), ((), ())), preferred_element_type=jnp.float32
    )


def step_kernel(
    features, cotangent, conv_weight, down_weight, up_weight, live_count, codes, dest, order,
    output, summed, block,
    own, grads, table, weight_t, stacked, pre_fine, mixed, rim, target_row, target_col, order_col,
    send_m, recv_m, send_g, recv_g, send_u, recv_u, joined, coarse_in, coarse_grad, returned, slope,
    sem_rs, sem_rr, sem_ms, sem_mr, sem_gs, sem_gr, sem_us, sem_ur, *sum_scratch,
):
    y, z, x, c = place()
    me = (z * 4 + x) * 2 + c
    slots, width = features.shape
    edge = slots // 8
    places, cap = send_m.shape[0], send_m.shape[1]
    group = 8
    span = group * cap
    bricks = coarse_in.shape[0]
    taps = codes.shape[0]
    sum_greet, sum_begin, sum_finish = reducer(block, summed, *sum_scratch)

    def at(device):
        return {"scene": y, "space": device}

    rim[...] = jnp.zeros_like(rim)
    barrier = pltpu.get_barrier_semaphore()

    def greet(k, carry):
        pl.semaphore_signal(
            barrier, inc=1, device_id=at((me + k) % places), device_id_type=MESH
        )
        return carry

    lax.fori_loop(1, places, greet, 0)
    sum_greet(barrier)

    count = live_count[0, 0]
    live = iota((slots, width), 0) < count
    zero_b = jnp.zeros((slots, width), jnp.bfloat16)
    own[...] = jnp.where(live, features[...], zero_b)
    grads[...] = jnp.where(live, cotangent[...], zero_b)

    goal = dest[...]
    named = goal == iota((places, slots), 0)
    named_b = one_hot(named)
    for part in range(3):
        cols = slice(part * 256, part * 256 + 256)
        earlier = one_hot(iota((slots, 256), 0) < iota((slots, 256), 1) + part * 256)
        before = dot(named_b, earlier)
        rank = jnp.sum(jnp.where(named[:, cols], before, 0.0), axis=0, keepdims=True)
        row = goal[:, cols].astype(jnp.float32) * cap + rank
        target_row[:, cols] = row
        target_col[cols, :] = jnp.broadcast_to(row, (128, 256)).T

    for part in range(12):
        cols = slice(part * 128, part * 128 + 128)
        order_col[cols, :] = jnp.broadcast_to(order[:, cols].astype(jnp.float32), (128, 128)).T

    pl.semaphore_wait(barrier, places - 1 + 23)

    def rim_copy(upward):
        start = edge if upward else 0
        there = 0 if upward else edge
        return pltpu.make_async_remote_copy(
            src_ref=features.at[pl.ds(start, edge), :], dst_ref=rim.at[pl.ds(there, edge), :],
            send_sem=sem_rs.at[1 - int(upward)], recv_sem=sem_rr.at[1 - int(upward)],
            device_id=at((me + (1 if upward else places - 1)) % places), device_id_type=MESH,
        )

    @pl.when(me < places - 1)
    def _():
        rim_copy(True).start()

    @pl.when(me > 0)
    def _():
        rim_copy(False).start()

    def exchange(sent, received, send_sems, recv_sems, device, source):
        return pltpu.make_async_remote_copy(
            src_ref=sent.at[device], dst_ref=received.at[source],
            send_sem=send_sems.at[device], recv_sem=recv_sems.at[source],
            device_id=at(device), device_id_type=MESH,
        )

    def send_group(which, sent, received, send_sems, recv_sems):
        def one(k, carry):
            device = which * group + (me + k) % group

            @pl.when(device != me)
            def _():
                exchange(sent, received, send_sems, recv_sems, device, me).start()

            return carry

        lax.fori_loop(0, group, one, 0)

    def in_order(j):
        odd = j % 2
        return (z + 4 - odd + (1 - 2 * odd) * (j // 2)) % 8

    def spread(rows, sent, received, send_sems, recv_sems):
        def one(j, carry):
            which = in_order(j)
            chosen = one_hot(
                (iota((span, slots), 0) + which * span).astype(jnp.float32) == target_row[...]
            )
            packed = dot(chosen, rows[...]).reshape(group, cap, width).astype(jnp.bfloat16)
            sent[pl.ds(which * group, group)] = packed
            send_group(which, sent, received, send_sems, recv_sems)
            return carry

        lax.fori_loop(0, places // group, one, 0)
        received[pl.ds(me, 1)] = sent[pl.ds(me, 1)]

    spread(grads, send_g, recv_g, sem_gs, sem_gr)

    def turn(k, carry):
        rows = pl.ds(pl.multiple_of(k * width, width), width)
        weight_t[:, rows] = conv_weight[rows, :].astype(jnp.float32).T.astype(jnp.bfloat16)
        return carry

    lax.fori_loop(0, taps + 1, turn, 0)
    for part in range(6):
        cols = slice(part * 128, part * 128 + 128)
        turned = own[cols, :].astype(jnp.float32).T.astype(jnp.bfloat16)
        table[:, cols] = turned
        stacked[0:width, cols] = turned

    def pick(k, part, depth):
        code = codes[pl.ds(k, 1), part * 256 : part * 256 + 256]
        chosen = one_hot(iota((depth, 256), 0) == code)
        found = dot(table[:, 0:depth], chosen).astype(jnp.bfloat16)
        rows = pl.ds(pl.multiple_of((k + 1) * width, width), width)
        stacked[rows, part * 256 : part * 256 + 256] = found

    def inner(k, carry):
        pick(k, 1, slots)
        pick(k, 2, slots)
        return carry

    lax.fori_loop(0, taps, inner, 0)

    @pl.when(me > 0)
    def _():
        rim_copy(True).wait_recv()

    @pl.when(me < places - 1)
    def _():
        rim_copy(False).wait_recv()

    table[:, slots:] = rim[...].astype(jnp.float32).T.astype(jnp.bfloat16)

    def outer(k, carry):
        pick(k, 0, slots + 256)
        return carry

    lax.fori_loop(0, taps, outer, 0)

    for part in range(3):
        cols = slice(part * 256, part * 256 + 256)
        pre = dot(weight_t[...], stacked[:, cols]).T
        pre_fine[cols, :] = pre
        alive = iota((256, width), 0) + part * 256 < count
        blend = jnp.where(alive, own[cols, :].astype(jnp.float32) + jax.nn.silu(pre), 0.0)
        mixed[cols, :] = blend.astype(jnp.bfloat16)

    spread(mixed, send_m, recv_m, sem_ms, sem_mr)

    def arrived(received, sent, send_sems, recv_sems):
        def one(k, carry):
            exchange(sent, received, send_sems, recv_sems, me, (me + k) % places).wait_recv()
            return carry

        lax.fori_loop(1, places, one, 0)

    def left(received, sent, send_sems, recv_sems):
        def one(k, carry):
            exchange(sent, received, send_sems, recv_sems, (me + k) % places, me).wait_send()
            return carry

        lax.fori_loop(1, places, one, 0)

    def flat(received, lanes, base):
        def one(j, carry):
            rows = pl.ds(pl.multiple_of(j * span, span), span)
            value = received[pl.ds(j * group, group)].astype(jnp.float32)
            joined[rows, base : base + lanes] = value.reshape(span, lanes).astype(jnp.bfloat16)
            return carry

        lax.fori_loop(0, places // group, one, 0)

    arrived(recv_g, send_g, sem_gs, sem_gr)
    flat(recv_g, width, width)
    arrived(recv_m, send_m, sem_ms, sem_mr)
    flat(recv_m, width, 0)

    received_rows = places * cap

    def bring(k, carry):
        rows = pl.ds(pl.multiple_of(k * bricks, bricks), bricks)
        cols = pl.ds(pl.multiple_of(k * width, width), width)
        chosen = one_hot(
            order_col[rows, 0:1] == iota((bricks, received_rows), 1).astype(jnp.float32)
        )
        pair = dot(chosen, joined[...]).astype(jnp.bfloat16)
        coarse_in[:, cols] = pair[:, 0:width]
        coarse_grad[:, cols] = pair[:, width:]
        return carry

    lax.fori_loop(0, 8, bring, 0)

    pre = dot(coarse_in[...], down_weight[...])
    coarse = jax.nn.silu(pre).astype(jnp.bfloat16)
    back = dot(coarse_grad[...], up_weight[...], 1, 1)
    grad_pre = (back * silu_grad(pre)).astype(jnp.bfloat16)
    up_rows = dot(coarse, up_weight[...]).astype(jnp.bfloat16)
    grad_in = dot(grad_pre, down_weight[...], 1, 1).astype(jnp.bfloat16)
    for k in range(8):
        rows = slice(k * bricks, k * bricks + bricks)
        returned[rows, 0:width] = up_rows[:, k * width : k * width + width]
        returned[rows, width:] = grad_in[:, k * width : k * width + width]

    def give(j, carry):
        which = in_order(j)
        chosen = one_hot(iota((span, received_rows), 0) + which * span == order[...])
        packed = dot(chosen, returned[...]).reshape(group, cap, 2 * width).astype(jnp.bfloat16)
        send_u[pl.ds(which * group, group)] = packed
        send_group(which, send_u, recv_u, sem_us, sem_ur)
        return carry

    lax.fori_loop(0, places // group, give, 0)
    recv_u[pl.ds(me, 1)] = send_u[pl.ds(me, 1)]

    deep, wide = down_weight.shape
    base = 4 * deep
    grad_down = dot(coarse_in[...], grad_pre, 0, 0)
    for k in range(wide // width):
        block[base + k * deep : base + (k + 1) * deep, :] = grad_down[:, k * width : k * width + width]
    base = base + deep * wide // width
    grad_up = dot(coarse, coarse_grad[...], 0, 0)
    for k in range(deep // width):
        block[base + k * wide : base + (k + 1) * wide, :] = grad_up[:, k * width : k * width + width]

    sum_begin()

    arrived(recv_u, send_u, sem_us, sem_ur)
    flat(recv_u, 2 * width, 0)

    def settle(part, carry):
        rows = pl.ds(pl.multiple_of(part * 256, 256), 256)
        chosen = one_hot(
            target_col[rows, 0:1] == iota((256, received_rows), 1).astype(jnp.float32)
        )
        fine = dot(chosen, joined[...])
        alive = iota((256, width), 0) + part * 256 < count
        total = mixed[rows, :].astype(jnp.float32) + fine[:, 0:width]
        output[rows, :] = jnp.where(alive, total, 0.0).astype(jnp.bfloat16)
        grad_mixed = jnp.where(alive, grads[rows, :].astype(jnp.float32) + fine[:, width:], 0.0)
        slope[rows, :] = (grad_mixed * silu_grad(pre_fine[rows, :])).astype(jnp.bfloat16)
        return carry

    lax.fori_loop(0, 3, settle, 0)

    def convolve(k, carry):
        rows = pl.ds(pl.multiple_of(k * 384, 384), 384)
        block[rows, :] = dot(stacked[rows, :], slope[...])
        return carry

    lax.fori_loop(0, 9, convolve, 0)
    block[27 * width : 4 * deep, :] = jnp.zeros((4 * deep - 27 * width, width), jnp.float32)
    sum_finish()

    left(recv_g, send_g, sem_gs, sem_gr)
    left(recv_m, send_m, sem_ms, sem_mr)
    left(recv_u, send_u, sem_us, sem_ur)

    @pl.when(me < places - 1)
    def _():
        rim_copy(True).wait_send()

    @pl.when(me > 0)
    def _():
        rim_copy(False).wait_send()


def whole_step(features, cotangent, conv_weight, down_weight, up_weight, live_count, codes, dest, order):
    slots, width = features.shape
    taps = codes.shape[0]
    deep, wide = down_weight.shape
    rows = order.shape[1]
    places = lax.axis_size("space")
    cap = rows // places
    bricks = rows // 8
    wire = jnp.bfloat16
    dma = pltpu.SemaphoreType.DMA
    vmem = pl.BlockSpec(memory_space=pltpu.VMEM)
    smem = pl.BlockSpec(memory_space=pltpu.SMEM)
    return pl.pallas_call(
        step_kernel,
        out_shape=(
            jax.ShapeDtypeStruct((slots, width), wire),
            jax.ShapeDtypeStruct((2, 16, deep // 4, width), wire),
        ),
        in_specs=[vmem, vmem, vmem, vmem, vmem, smem, vmem, vmem, vmem],
        out_specs=(vmem, vmem),
        scratch_shapes=[
            pltpu.VMEM((8 * deep, width), jnp.float32),
            pltpu.VMEM((slots, width), wire),
            pltpu.VMEM((slots, width), wire),
            pltpu.VMEM((width, slots + 256), wire),
            pltpu.VMEM((width, (taps + 1) * width), wire),
            pltpu.VMEM(((taps + 1) * width, slots), wire),
            pltpu.VMEM((slots, width), jnp.float32),
            pltpu.VMEM((slots, width), wire),
            pltpu.VMEM((256, width), wire),
            pltpu.VMEM((1, slots), jnp.float32),
            pltpu.VMEM((slots, 128), jnp.float32),
            pltpu.VMEM((rows, 128), jnp.float32),
            pltpu.VMEM((places, cap, width), wire),
            pltpu.VMEM((places, cap, width), wire),
            pltpu.VMEM((places, cap, width), wire),
            pltpu.VMEM((places, cap, width), wire),
            pltpu.VMEM((places, cap, 2 * width), wire),
            pltpu.VMEM((places, cap, 2 * width), wire),
            pltpu.VMEM((rows, 2 * width), wire),
            pltpu.VMEM((bricks, deep), wire),
            pltpu.VMEM((bricks, deep), wire),
            pltpu.VMEM((rows, 2 * width), wire),
            pltpu.VMEM((slots, width), wire),
            dma((2,)), dma((2,)), dma((places,)), dma((places,)), dma((places,)), dma((places,)),
            dma((places,)), dma((places,)),
            pltpu.VMEM((16, deep // 4, width), wire),
            pltpu.VMEM((16, deep // 4, width), wire),
            pltpu.VMEM((16, deep // 4, width), wire),
            pltpu.VMEM((16, deep // 4, width), wire),
            pltpu.VMEM((8, deep // 32, width), wire),
            pltpu.VMEM((8, deep // 32, width), wire),
            pltpu.VMEM((deep // 4, width), jnp.float32),
            dma((16,)), dma((16,)), dma((16,)), dma((16,)), dma((8,)), dma((8,)),
            dma((8,)), dma((8,)), dma((16,)), dma((16,)), dma((16,)), dma((16,)),
        ],
        compiler_params=pltpu.CompilerParams(collective_id=1, has_side_effects=True),
        name="brick_step",
    )(features, cotangent, conv_weight, down_weight, up_weight, live_count, codes, dest, order)


def on_device(
    features, cotangent, conv_weight, down_weight, up_weight, live_count, neighbours, destination, assemble
):
    slots, width = features.shape[1], features.shape[2]
    deep, wide = down_weight.shape
    taps = conv_weight.shape[0]
    order = assemble[0, 0].reshape(-1, 8).T.reshape(1, -1)
    output, summed = whole_step(
        features[0], cotangent[0], conv_weight, down_weight, up_weight, live_count,
        neighbours[0], destination[0].reshape(1, slots), order,
    )
    total = summed.reshape(-1, width)
    grad_conv = total[:taps].astype(jnp.float32)
    half = deep * wide // width
    down = total[deep * 4 : deep * 4 + half].reshape(wide // width, deep, width)
    up = total[deep * 4 + half :].reshape(deep // width, wide, width)
    grad_down = down.transpose(1, 0, 2).reshape(deep, wide).astype(jnp.float32)
    grad_up = up.transpose(1, 0, 2).reshape(wide, deep).astype(jnp.float32)
    return (output[None], grad_conv, grad_down, grad_up)


def solution(mesh):
    in_specs = (
        P("scene", "space", None),
        P("scene", "space", None),
        P(),
        P(),
        P(),
        P("scene", "space"),
        P("scene", None, "space"),
        P("scene", "space", None),
        P("scene", "space", None),
    )
    out_specs = (P("scene", "space", None), P(), P(), P())
    return jax.shard_map(
        on_device, mesh=mesh, in_specs=in_specs, out_specs=out_specs, check_vma=False
    )
```
